32 devices in a mesh: tiles: 2 (over x), space: 8 (over z, y), chan: 2 (over core).
Axes of the slice: x: 2, y: 2, z: 4, core: 2. Of those that a mesh axis runs over, the one named last changes fastest.
Arguments:
- volume: bfloat16 [32, 64, 32, 256], P(None, 'space', 'tiles', 'chan'), parts along dimension 2, may hold values from -6 to 6
- weight_one: bfloat16 [3, 3, 3, 256, 256], replicated, may hold values from -0.078125 to 0.078125
- bias_one: float32 [256], replicated, may hold values from -3 to 3
- weight_two: bfloat16 [3, 3, 3, 256, 256], replicated, may hold values from -0.078125 to 0.078125
- bias_two: float32 [256], replicated, may hold values from -3 to 3
Outputs:
- features: bfloat16 [32, 64, 32, 256], P('space', None, 'tiles', 'chan'), parts along dimension 2
The draws below stay inside these ranges and needn't reach their ends.
There are 2 independent parts, one for each index of `tiles`. The reference program is written for one: setup_inputs(seed, part) draws one part's arguments, and reference() takes and returns one part's arrays. A program takes and returns all parts, laid end to end along the dimension named above; an argument that names none is the same for every part. Nothing has to cross between parts.
All inputs are finite; a program needn't handle non-finite values.
Results may differ from the reference program's by a relative error of at most 0.0044.
Values may be sent and summed in bfloat16 or wider, within the bound.
A program may use at most 128 MiB of HBM per device.

```python
import jax
import jax.numpy as jnp
from jax import lax

C = 256
ZC = 16
X = 32
Y = 64


def block_levels(rng, extent, cuts, smallest, largest):
    factor_of, own = 1.0, jax.random.fold_in(rng, 6)
    for position, blocks in cuts:
        heights = jnp.exp(jax.random.uniform(jax.random.fold_in(own, position), (blocks,), jnp.float32, smallest / len(cuts), largest / len(cuts)))
        factor_of = factor_of * jnp.repeat(heights, extent[position] // blocks).reshape([-1 if axis == position else 1 for axis in range(len(extent))])
    return factor_of


def bell_draw(own_key, shape, deviation, bound, shards=(), kind=jnp.bfloat16):
    gain = block_levels(own_key, shape, shards, -0.22, 0.18) if shards else 1.0
    drawn = jax.random.normal(own_key, shape, jnp.float32) * deviation * gain
    return jnp.minimum(jnp.maximum(drawn, -bound), bound).astype(kind)


def setup_inputs(seed: int = 0, part: int = 0) -> dict:
    key_list = jax.random.split(jax.random.key(seed), 6)
    part_keys = jax.random.split(jax.random.fold_in(key_list[5], part), 6)
    volume = bell_draw(part_keys[0], (X, Y, ZC, C), 1.0, 6.0, ((1, 8), (3, 2)))
    weight_one = bell_draw(key_list[1], (3, 3, 3, C, C), (27 * C) ** -0.5, 0.078125)
    bias_one = bell_draw(key_list[2], (C,), 0.5, 3.0, (), jnp.float32)
    weight_two = bell_draw(key_list[3], (3, 3, 3, C, C), (27 * C) ** -0.5, 0.078125)
    bias_two = bell_draw(key_list[4], (C,), 0.5, 3.0, (), jnp.float32)
    return {"volume": volume, "weight_one": weight_one, "bias_one": bias_one, "weight_two": weight_two, "bias_two": bias_two}


def convolve(field, kernel, bias):
    result = lax.conv_general_dilated(field.astype(jnp.float32)[None], kernel.astype(jnp.float32), (1, 1, 1), ((1, 1), (1, 1), (1, 1)), dimension_numbers=("NDHWC", "DHWIO", "NDHWC"), precision=lax.Precision.HIGHEST)[0]
    return result + bias


def reference(volume, weight_one, bias_one, weight_two, bias_two):
    hidden = jnp.maximum(convolve(volume, weight_one, bias_one), 0.0).astype(jnp.bfloat16)
    return jnp.maximum(convolve(hidden, weight_two, bias_two), 0.0).astype(jnp.bfloat16)
```

```python
import functools

import jax
import jax.numpy as jnp
from jax import lax
from jax.experimental import pallas as pl
from jax.experimental.pallas import tpu as pltpu
from jax.sharding import PartitionSpec as P

MESH = pl.DeviceIdType.MESH
CHUNK = 2


def kernel(
    slabs, vol, w1_hbm, w2_hbm, bias1, bias2, out,
    xbuf, hid, w1, w2, obuf,
    wsem, lsem, psend, precv, hsend, hrecv, osend, orecv, olocal,
):
    s, c = lax.axis_index("space"), lax.axis_index("chan")
    other = 1 - c
    rows, yb, zc, share = vol.shape
    half = rows // 2
    slab = out.shape[0]
    nb = half // slab
    nq = (half + 4) // CHUNK
    nu = (half + 2) // CHUNK

    def dev(space, chan):
        return {"space": space, "chan": chan}

    load1 = pltpu.make_async_copy(w1_hbm, w1, wsem.at[0])
    load2 = pltpu.make_async_copy(w2_hbm, w2, wsem.at[1])
    load1.start()
    load2.start()

    barrier = pltpu.get_barrier_semaphore()

    def greet(i, carry):
        @pl.when(i != s)
        def _():
            for chan in range(2):
                pl.semaphore_signal(
                    barrier, inc=1, device_id=dev(i, chan), device_id_type=MESH
                )
        return carry

    lax.fori_loop(0, slabs, greet, 0)
    pl.semaphore_signal(barrier, inc=1, device_id=dev(s, other), device_id_type=MESH)

    edge = jnp.zeros((2, 2) + xbuf.shape[2:], xbuf.dtype)

    @pl.when(c == 0)
    def _():
        xbuf[:, 0:2] = edge

    @pl.when(c == 1)
    def _():
        xbuf[:, half + 2 : half + 4] = edge

    side = jnp.zeros((2, half + 4, 2, zc, share), xbuf.dtype)

    @pl.when(s == 0)
    def _():
        xbuf[:, :, 0:2] = side

    @pl.when(s == slabs - 1)
    def _():
        xbuf[:, :, yb + 2 : yb + 4] = side

    pl.semaphore_wait(barrier, 2 * slabs - 1)

    def first_block(space):
        return lax.rem(space + nb // 2, nb)

    def order(k, start, count):
        return jnp.where(start + k < count, start + k, count - 1 - k)

    def valid(q, chan):
        return jnp.where(chan == 0, q >= 1, q <= nq - 2)

    def source(q, chan):
        return pl.ds(chan * half + CHUNK * q - 2, CHUNK)

    def target(q):
        return pl.ds(CHUNK * q, CHUNK)

    def local_in(q):
        return pltpu.make_async_copy(
            vol.at[source(q, c)], xbuf.at[c, target(q), pl.ds(2, yb)], lsem.at[q]
        )

    def partner_in(q):
        return pltpu.make_async_remote_copy(
            src_ref=vol.at[source(q, other)],
            dst_ref=xbuf.at[c, target(q), pl.ds(2, yb)],
            send_sem=psend.at[q],
            recv_sem=precv.at[q],
            device_id=dev(s, other),
            device_id_type=MESH,
        )

    def partner_arrival(q):
        return pltpu.make_async_remote_copy(
            src_ref=xbuf.at[other, target(q), pl.ds(2, yb)],
            dst_ref=xbuf.at[other, target(q), pl.ds(2, yb)],
            send_sem=psend.at[q],
            recv_sem=precv.at[q],
            device_id=dev(s, other),
            device_id_type=MESH,
        )

    def halo_in(q, way, chan):
        return pltpu.make_async_remote_copy(
            src_ref=vol.at[source(q, chan), pl.ds((1 - way) * (yb - 2), 2)],
            dst_ref=xbuf.at[c, target(q), pl.ds(way * (yb + 2), 2)],
            send_sem=hsend.at[way, chan, q],
            recv_sem=hrecv.at[way, c, q],
            device_id=dev(s + 1 - 2 * way, chan),
            device_id_type=MESH,
        )

    def halo_arrival(q, way, chan):
        region = xbuf.at[chan, target(q), pl.ds(way * (yb + 2), 2)]
        return pltpu.make_async_remote_copy(
            src_ref=region,
            dst_ref=region,
            send_sem=hsend.at[way, chan, q],
            recv_sem=hrecv.at[way, chan, q],
            device_id=dev(s, other),
            device_id_type=MESH,
        )

    def has(way):
        return s < slabs - 1 if way == 0 else s > 0

    def send_inputs(k, carry):
        q = order(k, 2 * first_block(s), nq)

        @pl.when(valid(q, c))
        def _():
            local_in(q).start()

        @pl.when(valid(q, other))
        def _():
            partner_in(q).start()

        for way in range(2):
            @pl.when(has(way))
            def _():
                there = order(k, 2 * first_block(s + 1 - 2 * way), nq)
                for chan in range(2):
                    @pl.when(valid(there, chan))
                    def _():
                        halo_in(there, way, chan).start()
        return carry

    lax.fori_loop(0, nq, send_inputs, 0)

    def await_chunk(q):
        @pl.when(valid(q, c))
        def _():
            local_in(q).wait()
            partner_arrival(q).wait_recv()
            for way in range(2):
                @pl.when(has(1 - way))
                def _():
                    for chan in range(2):
                        halo_arrival(q, way, chan).wait_recv()

    def shifted(total, count):
        z = lax.rem(lax.broadcasted_iota(jnp.int32, (count, 1), 0), zc)
        low = jnp.where(z == 0, 0.0, pltpu.roll(total(0), 1, 0))
        high = jnp.where(z == zc - 1, 0.0, pltpu.roll(total(2), count - 1, 0))
        return total(1) + low + high

    def convolve(pieces, weight, bias, count):
        lhs = jnp.concatenate([piece.reshape(count, -1) for piece in pieces], axis=1)
        depth = lhs.shape[1]

        def total(tap):
            rhs = weight[:, :, tap].reshape(depth, weight.shape[-1])
            return jnp.dot(lhs, rhs, preferred_element_type=jnp.float32)

        return jnp.maximum(shifted(total, count) + bias[...], 0.0).astype(jnp.bfloat16)

    def hidden_unit(u):
        r = CHUNK * u
        result = convolve(
            [
                xbuf[h, pl.ds(r + a, CHUNK), b : b + yb + 2]
                for a in range(3)
                for b in range(3)
                for h in range(2)
            ],
            w1, bias1, CHUNK * (yb + 2) * zc,
        )
        hid[pl.ds(r, CHUNK)] = result.reshape(CHUNK, yb + 2, zc, hid.shape[-1])
        line = jnp.zeros((CHUNK, zc, hid.shape[-1]), hid.dtype)

        @pl.when(s == 0)
        def _():
            hid[pl.ds(r, CHUNK), 0] = line

        @pl.when(s == slabs - 1)
        def _():
            hid[pl.ds(r, CHUNK), yb + 1] = line

        plane = jnp.zeros(hid.shape[1:], hid.dtype)

        @pl.when((c == 0) & (u == 0))
        def _():
            hid[0] = plane

        @pl.when((c == 1) & (u == nu - 1))
        def _():
            hid[half + 1] = plane

    start = first_block(s)
    await_chunk(2 * start)
    load1.wait()

    def hidden_step(j):
        u = order(j, 2 * start, nu)
        await_chunk(jnp.where(2 * start + j < nu, u + 1, u))
        hidden_unit(u)

    def out_remote(b, chan):
        return pltpu.make_async_remote_copy(
            src_ref=obuf.at[b, chan],
            dst_ref=out.at[:, pl.ds(yb * s, yb)],
            send_sem=osend.at[b, chan],
            recv_sem=orecv.at[s],
            device_id=dev(nb * c + b, chan),
            device_id_type=MESH,
        )

    def out_local(b):
        return pltpu.make_async_copy(
            obuf.at[b, c], out.at[:, pl.ds(yb * s, yb)], olocal
        )

    def away(b, chan):
        return (nb * c + b != s) | (chan != c)

    def block_step(k, carry):
        lax.fori_loop(
            2 * k + jnp.where(k == 0, 0, 1), 2 * k + 3,
            lambda j, x: (hidden_step(j), x)[1], 0,
        )

        @pl.when(k == 0)
        def _():
            load2.wait()

        b = order(k, start, nb)
        result = convolve(
            [
                hid[pl.ds(slab * b + a, slab), e : e + yb]
                for a in range(3)
                for e in range(3)
            ],
            w2, bias2, slab * yb * zc,
        )
        for chan in range(2):
            obuf[b, chan] = result[:, chan * share : (chan + 1) * share].reshape(
                slab, yb, zc, share
            )
        for chan in range(2):
            @pl.when(away(b, chan))
            def _():
                out_remote(b, chan).start()

        @pl.when(nb * c + b == s)
        def _():
            out_local(b).start()
        return carry

    lax.fori_loop(0, nb, block_step, 0)

    def sent_inputs(q, carry):
        @pl.when(valid(q, other))
        def _():
            partner_in(q).wait_send()

        for way in range(2):
            @pl.when(has(way))
            def _():
                for chan in range(2):
                    @pl.when(valid(q, chan))
                    def _():
                        halo_in(q, way, chan).wait_send()
        return carry

    lax.fori_loop(0, nq, sent_inputs, 0)

    def sent_outputs(b, carry):
        for chan in range(2):
            @pl.when(away(b, chan))
            def _():
                out_remote(b, chan).wait_send()

        @pl.when(nb * c + b == s)
        def _():
            out_local(b).wait()
        return carry

    lax.fori_loop(0, nb, sent_outputs, 0)

    def arrived(i, carry):
        @pl.when((i != s) | (s // nb != c))
        def _():
            region = out.at[:, pl.ds(yb * i, yb)]
            pltpu.make_async_remote_copy(
                src_ref=region,
                dst_ref=region,
                send_sem=osend.at[0, 0],
                recv_sem=orecv.at[i],
                device_id=dev(s, other),
                device_id_type=MESH,
            ).wait_recv()
        return carry

    lax.fori_loop(0, slabs, arrived, 0)


def body(slabs, volume, weight_one, bias_one, weight_two, bias_two):
    rows, yb, zc, share = volume.shape
    half, slab = rows // 2, rows // slabs
    nb = half // slab
    nq = (half + 4) // CHUNK
    channels = weight_one.shape[-1]
    anywhere = pl.BlockSpec(memory_space=pl.ANY)
    vmem = pl.BlockSpec(memory_space=pltpu.VMEM)
    dma = pltpu.SemaphoreType.DMA
    kind = volume.dtype
    return pl.pallas_call(
        functools.partial(kernel, slabs),
        out_shape=jax.ShapeDtypeStruct((slab, yb * slabs, zc, share), kind),
        in_specs=[anywhere, anywhere, anywhere, vmem, vmem],
        out_specs=anywhere,
        scratch_shapes=[
            pltpu.VMEM((2, half + 4, yb + 4, zc, share), kind),
            pltpu.VMEM((half + 2, yb + 2, zc, channels), kind),
            pltpu.VMEM(weight_one.shape, kind),
            pltpu.VMEM(weight_two.shape, kind),
            pltpu.VMEM((nb, 2, slab, yb, zc, share), kind),
            dma((2,)),
            dma((nq,)),
            dma((nq,)),
            dma((nq,)),
            dma((2, 2, nq)),
            dma((2, 2, nq)),
            dma((nb, 2)),
            dma((slabs,)),
            dma,
        ],
        compiler_params=pltpu.CompilerParams(
            collective_id=0, has_side_effects=True, vmem_limit_bytes=58 * 2**20
        ),
    )(volume, weight_one, weight_two, bias_one[None], bias_two[None])


def solution(mesh):
    return jax.shard_map(
        functools.partial(body, mesh.shape["space"]),
        mesh=mesh,
        in_specs=(P(None, "space", "tiles", "chan"), P(), P(), P(), P()),
        out_specs=P("space", None, "tiles", "chan"),
        check_vma=False,
    )
```

```python
import functools

import jax
import jax.numpy as jnp
from jax import lax
from jax.experimental import pallas as pl
from jax.experimental.pallas import tpu as pltpu
from jax.sharding import PartitionSpec as P

MESH = pl.DeviceIdType.MESH
CHUNK = 2


def kernel(
    slabs, vol, w1_hbm, w2_hbm, bias1, bias2, out,
    xbuf, hid, w1, w2, obuf,
    wsem, lsem, psend, precv, hsend, hrecv, osend, orecv, olocal,
):
    s, c = lax.axis_index("space"), lax.axis_index("chan")
    other = 1 - c
    rows, yb, zc, share = vol.shape
    half = rows // 2
    slab = out.shape[0]
    nb = half // slab
    nq = (half + 4) // CHUNK
    nu = (half + 2) // CHUNK

    def dev(space, chan):
        return {"space": space, "chan": chan}

    load1 = pltpu.make_async_copy(w1_hbm, w1, wsem.at[0])
    load2 = pltpu.make_async_copy(w2_hbm, w2, wsem.at[1])
    load1.start()
    load2.start()

    barrier = pltpu.get_barrier_semaphore()

    def greet(i, carry):
        @pl.when(i != s)
        def _():
            for chan in range(2):
                pl.semaphore_signal(
                    barrier, inc=1, device_id=dev(i, chan), device_id_type=MESH
                )
        return carry

    lax.fori_loop(0, slabs, greet, 0)
    pl.semaphore_signal(barrier, inc=1, device_id=dev(s, other), device_id_type=MESH)

    edge = jnp.zeros((2, 2) + xbuf.shape[2:], xbuf.dtype)

    @pl.when(c == 0)
    def _():
        xbuf[:, 0:2] = edge

    @pl.when(c == 1)
    def _():
        xbuf[:, half + 2 : half + 4] = edge

    side = jnp.zeros((2, half + 4, 2, zc, share), xbuf.dtype)

    @pl.when(s == 0)
    def _():
        xbuf[:, :, 0:2] = side

    @pl.when(s == slabs - 1)
    def _():
        xbuf[:, :, yb + 2 : yb + 4] = side

    pl.semaphore_wait(barrier, 2 * slabs - 1)

    def first_block(space):
        return lax.rem(space // 2 + nb // 2 + lax.rem(space, 2) * (nb // 2), nb)

    def order(k, start, count):
        return jnp.where(start + k < count, start + k, count - 1 - k)

    def valid(q, chan):
        return jnp.where(chan == 0, q >= 1, q <= nq - 2)

    def source(q, chan):
        return pl.ds(chan * half + CHUNK * q - 2, CHUNK)

    def target(q):
        return pl.ds(CHUNK * q, CHUNK)

    def local_in(q):
        return pltpu.make_async_copy(
            vol.at[source(q, c)], xbuf.at[c, target(q), pl.ds(2, yb)], lsem.at[q]
        )

    def partner_in(q):
        return pltpu.make_async_remote_copy(
            src_ref=vol.at[source(q, other)],
            dst_ref=xbuf.at[c, target(q), pl.ds(2, yb)],
            send_sem=psend.at[q],
            recv_sem=precv.at[q],
            device_id=dev(s, other),
            device_id_type=MESH,
        )

    def partner_arrival(q):
        return pltpu.make_async_remote_copy(
            src_ref=xbuf.at[other, target(q), pl.ds(2, yb)],
            dst_ref=xbuf.at[other, target(q), pl.ds(2, yb)],
            send_sem=psend.at[q],
            recv_sem=precv.at[q],
            device_id=dev(s, other),
            device_id_type=MESH,
        )

    def halo_in(q, way, chan):
        return pltpu.make_async_remote_copy(
            src_ref=vol.at[source(q, chan), pl.ds((1 - way) * (yb - 2), 2)],
            dst_ref=xbuf.at[c, target(q), pl.ds(way * (yb + 2), 2)],
            send_sem=hsend.at[way, chan, q],
            recv_sem=hrecv.at[way, c, q],
            device_id=dev(s + 1 - 2 * way, chan),
            device_id_type=MESH,
        )

    def halo_arrival(q, way, chan):
        region = xbuf.at[chan, target(q), pl.ds(way * (yb + 2), 2)]
        return pltpu.make_async_remote_copy(
            src_ref=region,
            dst_ref=region,
            send_sem=hsend.at[way, chan, q],
            recv_sem=hrecv.at[way, chan, q],
            device_id=dev(s, other),
            device_id_type=MESH,
        )

    def has(way):
        return s < slabs - 1 if way == 0 else s > 0

    def send_inputs(k, carry):
        q = order(k, 2 * first_block(s), nq)

        @pl.when(valid(q, c))
        def _():
            local_in(q).start()

        @pl.when(valid(q, other))
        def _():
            partner_in(q).start()

        for way in range(2):
            @pl.when(has(way))
            def _():
                there = order(k, 2 * first_block(s + 1 - 2 * way), nq)
                for chan in range(2):
                    @pl.when(valid(there, chan))
                    def _():
                        halo_in(there, way, chan).start()
        return carry

    lax.fori_loop(0, 5, send_inputs, 0)

    def await_chunk(q):
        @pl.when(valid(q, c))
        def _():
            local_in(q).wait()
            partner_arrival(q).wait_recv()
            for way in range(2):
                @pl.when(has(1 - way))
                def _():
                    for chan in range(2):
                        halo_arrival(q, way, chan).wait_recv()

    def shifted(total, count):
        z = lax.rem(lax.broadcasted_iota(jnp.int32, (count, 1), 0), zc)
        low = jnp.where(z == 0, 0.0, pltpu.roll(total(0), 1, 0))
        high = jnp.where(z == zc - 1, 0.0, pltpu.roll(total(2), count - 1, 0))
        return total(1) + low + high

    def convolve(pieces, weight, bias, count):
        lhs = jnp.concatenate([piece.reshape(count, -1) for piece in pieces], axis=1)
        depth = lhs.shape[1]

        def total(tap):
            rhs = weight[:, :, tap].reshape(depth, weight.shape[-1])
            return jnp.dot(lhs, rhs, preferred_element_type=jnp.float32)

        return jnp.maximum(shifted(total, count) + bias[...], 0.0).astype(jnp.bfloat16)

    def hidden_unit(u):
        r = CHUNK * u
        result = convolve(
            [
                xbuf[h, pl.ds(r + a, CHUNK), b : b + yb + 2]
                for a in range(3)
                for b in range(3)
                for h in range(2)
            ],
            w1, bias1, CHUNK * (yb + 2) * zc,
        )
        hid[pl.ds(r, CHUNK)] = result.reshape(CHUNK, yb + 2, zc, hid.shape[-1])
        line = jnp.zeros((CHUNK, zc, hid.shape[-1]), hid.dtype)

        @pl.when(s == 0)
        def _():
            hid[pl.ds(r, CHUNK), 0] = line

        @pl.when(s == slabs - 1)
        def _():
            hid[pl.ds(r, CHUNK), yb + 1] = line

        plane = jnp.zeros(hid.shape[1:], hid.dtype)

        @pl.when((c == 0) & (u == 0))
        def _():
            hid[0] = plane

        @pl.when((c == 1) & (u == nu - 1))
        def _():
            hid[half + 1] = plane

    start = first_block(s)
    await_chunk(2 * start)
    load1.wait()

    def hidden_step(j):
        @pl.when(j + 5 < nq)
        def _():
            send_inputs(j + 5, 0)

        u = order(j, 2 * start, nu)
        await_chunk(jnp.where(2 * start + j < nu, u + 1, u))
        hidden_unit(u)

    def out_remote(b, chan):
        return pltpu.make_async_remote_copy(
            src_ref=obuf.at[b, chan],
            dst_ref=out.at[:, pl.ds(yb * s, yb)],
            send_sem=osend.at[b, chan],
            recv_sem=orecv.at[s],
            device_id=dev(nb * c + b, chan),
            device_id_type=MESH,
        )

    def out_local(b):
        return pltpu.make_async_copy(
            obuf.at[b, c], out.at[:, pl.ds(yb * s, yb)], olocal
        )

    def away(b, chan):
        return (nb * c + b != s) | (chan != c)

    def block_step(k, carry):
        lax.fori_loop(
            2 * k + jnp.where(k == 0, 0, 1), 2 * k + 3,
            lambda j, x: (hidden_step(j), x)[1], 0,
        )

        @pl.when(k == 0)
        def _():
            load2.wait()

        b = order(k, start, nb)
        result = convolve(
            [
                hid[pl.ds(slab * b + a, slab), e : e + yb]
                for a in range(3)
                for e in range(3)
            ],
            w2, bias2, slab * yb * zc,
        )
        for chan in range(2):
            obuf[b, chan] = result[:, chan * share : (chan + 1) * share].reshape(
                slab, yb, zc, share
            )
        for chan in range(2):
            @pl.when(away(b, chan))
            def _():
                out_remote(b, chan).start()

        @pl.when(nb * c + b == s)
        def _():
            out_local(b).start()
        return carry

    lax.fori_loop(0, nb, block_step, 0)

    def sent_inputs(q, carry):
        @pl.when(valid(q, other))
        def _():
            partner_in(q).wait_send()

        for way in range(2):
            @pl.when(has(way))
            def _():
                for chan in range(2):
                    @pl.when(valid(q, chan))
                    def _():
                        halo_in(q, way, chan).wait_send()
        return carry

    lax.fori_loop(0, nq, sent_inputs, 0)

    def sent_outputs(b, carry):
        for chan in range(2):
            @pl.when(away(b, chan))
            def _():
                out_remote(b, chan).wait_send()

        @pl.when(nb * c + b == s)
        def _():
            out_local(b).wait()
        return carry

    lax.fori_loop(0, nb, sent_outputs, 0)

    def arrived(i, carry):
        @pl.when((i != s) | (s // nb != c))
        def _():
            region = out.at[:, pl.ds(yb * i, yb)]
            pltpu.make_async_remote_copy(
                src_ref=region,
                dst_ref=region,
                send_sem=osend.at[0, 0],
                recv_sem=orecv.at[i],
                device_id=dev(s, other),
                device_id_type=MESH,
            ).wait_recv()
        return carry

    lax.fori_loop(0, slabs, arrived, 0)


def body(slabs, volume, weight_one, bias_one, weight_two, bias_two):
    rows, yb, zc, share = volume.shape
    half, slab = rows // 2, rows // slabs
    nb = half // slab
    nq = (half + 4) // CHUNK
    channels = weight_one.shape[-1]
    anywhere = pl.BlockSpec(memory_space=pl.ANY)
    vmem = pl.BlockSpec(memory_space=pltpu.VMEM)
    dma = pltpu.SemaphoreType.DMA
    kind = volume.dtype
    return pl.pallas_call(
        functools.partial(kernel, slabs),
        out_shape=jax.ShapeDtypeStruct((slab, yb * slabs, zc, share), kind),
        in_specs=[anywhere, anywhere, anywhere, vmem, vmem],
        out_specs=anywhere,
        scratch_shapes=[
            pltpu.VMEM((2, half + 4, yb + 4, zc, share), kind),
            pltpu.VMEM((half + 2, yb + 2, zc, channels), kind),
            pltpu.VMEM(weight_one.shape, kind),
            pltpu.VMEM(weight_two.shape, kind),
            pltpu.VMEM((nb, 2, slab, yb, zc, share), kind),
            dma((2,)),
            dma((nq,)),
            dma((nq,)),
            dma((nq,)),
            dma((2, 2, nq)),
            dma((2, 2, nq)),
            dma((nb, 2)),
            dma((slabs,)),
            dma,
        ],
        compiler_params=pltpu.CompilerParams(
            collective_id=0, has_side_effects=True, vmem_limit_bytes=58 * 2**20
        ),
    )(volume, weight_one, weight_two, bias_one[None], bias_two[None])


def solution(mesh):
    return jax.shard_map(
        functools.partial(body, mesh.shape["space"]),
        mesh=mesh,
        in_specs=(P(None, "space", "tiles", "chan"), P(), P(), P(), P()),
        out_specs=P("space", None, "tiles", "chan"),
        check_vma=False,
    )
```

```python
import functools

import jax
import jax.numpy as jnp
from jax import lax
from jax.experimental import pallas as pl
from jax.experimental.pallas import tpu as pltpu
from jax.sharding import PartitionSpec as P

MESH = pl.DeviceIdType.MESH
CHUNK = 2


def kernel(
    slabs, vol, w1_hbm, w2_hbm, bias1, bias2, out,
    xbuf, hid, w1, w2, obuf,
    wsem, lsem, psend, precv, hsend, hrecv, osend, orecv, olocal,
):
    s, c = lax.axis_index("space"), lax.axis_index("chan")
    other = 1 - c
    rows, yb, zc, share = vol.shape
    half = rows // 2
    slab = out.shape[0]
    nb = half // slab
    nq = (half + 4) // CHUNK
    nu = (half + 2) // CHUNK

    def dev(space, chan):
        return {"space": space, "chan": chan}

    load1 = pltpu.make_async_copy(w1_hbm, w1, wsem.at[0])
    load2 = pltpu.make_async_copy(w2_hbm, w2, wsem.at[1])
    load1.start()
    load2.start()

    barrier = pltpu.get_barrier_semaphore()

    def greet(i, carry):
        @pl.when(i != s)
        def _():
            for chan in range(2):
                pl.semaphore_signal(
                    barrier, inc=1, device_id=dev(i, chan), device_id_type=MESH
                )
        return carry

    lax.fori_loop(0, slabs, greet, 0)
    pl.semaphore_signal(barrier, inc=1, device_id=dev(s, other), device_id_type=MESH)

    edge = jnp.zeros((2, 2) + xbuf.shape[2:], xbuf.dtype)

    @pl.when(c == 0)
    def _():
        xbuf[:, 0:2] = edge

    @pl.when(c == 1)
    def _():
        xbuf[:, half + 2 : half + 4] = edge

    side = jnp.zeros((2, half + 4, 2, zc, share), xbuf.dtype)

    @pl.when(s == 0)
    def _():
        xbuf[:, :, 0:2] = side

    @pl.when(s == slabs - 1)
    def _():
        xbuf[:, :, yb + 2 : yb + 4] = side

    pl.semaphore_wait(barrier, 2 * slabs - 1)

    def first_block(space):
        return lax.rem(space // 2 + nb // 2 + lax.rem(space, 2), nb)

    def order(k, start, count):
        return jnp.where(start + k < count, start + k, count - 1 - k)

    def valid(q, chan):
        return jnp.where(chan == 0, q >= 1, q <= nq - 2)

    def source(q, chan):
        return pl.ds(chan * half + CHUNK * q - 2, CHUNK)

    def target(q):
        return pl.ds(CHUNK * q, CHUNK)

    def local_in(q):
        return pltpu.make_async_copy(
            vol.at[source(q, c)], xbuf.at[c, target(q), pl.ds(2, yb)], lsem.at[q]
        )

    def partner_in(q):
        return pltpu.make_async_remote_copy(
            src_ref=vol.at[source(q, other)],
            dst_ref=xbuf.at[c, target(q), pl.ds(2, yb)],
            send_sem=psend.at[q],
            recv_sem=precv.at[q],
            device_id=dev(s, other),
            device_id_type=MESH,
        )

    def partner_arrival(q):
        return pltpu.make_async_remote_copy(
            src_ref=xbuf.at[other, target(q), pl.ds(2, yb)],
            dst_ref=xbuf.at[other, target(q), pl.ds(2, yb)],
            send_sem=psend.at[q],
            recv_sem=precv.at[q],
            device_id=dev(s, other),
            device_id_type=MESH,
        )

    def halo_in(q, way, chan):
        return pltpu.make_async_remote_copy(
            src_ref=vol.at[source(q, chan), pl.ds((1 - way) * (yb - 2), 2)],
            dst_ref=xbuf.at[c, target(q), pl.ds(way * (yb + 2), 2)],
            send_sem=hsend.at[way, chan, q],
            recv_sem=hrecv.at[way, c, q],
            device_id=dev(s + 1 - 2 * way, chan),
            device_id_type=MESH,
        )

    def halo_arrival(q, way, chan):
        region = xbuf.at[chan, target(q), pl.ds(way * (yb + 2), 2)]
        return pltpu.make_async_remote_copy(
            src_ref=region,
            dst_ref=region,
            send_sem=hsend.at[way, chan, q],
            recv_sem=hrecv.at[way, chan, q],
            device_id=dev(s, other),
            device_id_type=MESH,
        )

    def has(way):
        return s < slabs - 1 if way == 0 else s > 0

    def send_inputs(k, carry):
        q = order(k, 2 * first_block(s), nq)

        @pl.when(valid(q, c))
        def _():
            local_in(q).start()

        @pl.when(valid(q, other))
        def _():
            partner_in(q).start()

        for way in range(2):
            @pl.when(has(way))
            def _():
                there = order(k, 2 * first_block(s + 1 - 2 * way), nq)
                for chan in range(2):
                    @pl.when(valid(there, chan))
                    def _():
                        halo_in(there, way, chan).start()
        return carry

    lax.fori_loop(0, 5, send_inputs, 0)

    def await_chunk(q):
        @pl.when(valid(q, c))
        def _():
            local_in(q).wait()
            partner_arrival(q).wait_recv()
            for way in range(2):
                @pl.when(has(1 - way))
                def _():
                    for chan in range(2):
                        halo_arrival(q, way, chan).wait_recv()

    def shifted(total, count):
        z = lax.rem(lax.broadcasted_iota(jnp.int32, (count, 1), 0), zc)
        low = jnp.where(z == 0, 0.0, pltpu.roll(total(0), 1, 0))
        high = jnp.where(z == zc - 1, 0.0, pltpu.roll(total(2), count - 1, 0))
        return total(1) + low + high

    def convolve(pieces, weight, bias, count):
        lhs = jnp.concatenate([piece.reshape(count, -1) for piece in pieces], axis=1)
        depth = lhs.shape[1]

        def total(tap):
            rhs = weight[:, :, tap].reshape(depth, weight.shape[-1])
            return jnp.dot(lhs, rhs, preferred_element_type=jnp.float32)

        return jnp.maximum(shifted(total, count) + bias[...], 0.0).astype(jnp.bfloat16)

    def hidden_unit(u):
        r = CHUNK * u
        result = convolve(
            [
                xbuf[h, pl.ds(r + a, CHUNK), b : b + yb + 2]
                for a in range(3)
                for b in range(3)
                for h in range(2)
            ],
            w1, bias1, CHUNK * (yb + 2) * zc,
        )
        hid[pl.ds(r, CHUNK)] = result.reshape(CHUNK, yb + 2, zc, hid.shape[-1])
        line = jnp.zeros((CHUNK, zc, hid.shape[-1]), hid.dtype)

        @pl.when(s == 0)
        def _():
            hid[pl.ds(r, CHUNK), 0] = line

        @pl.when(s == slabs - 1)
        def _():
            hid[pl.ds(r, CHUNK), yb + 1] = line

        plane = jnp.zeros(hid.shape[1:], hid.dtype)

        @pl.when((c == 0) & (u == 0))
        def _():
            hid[0] = plane

        @pl.when((c == 1) & (u == nu - 1))
        def _():
            hid[half + 1] = plane

    start = first_block(s)
    await_chunk(2 * start)
    load1.wait()

    def hidden_step(j):
        @pl.when(j + 5 < nq)
        def _():
            send_inputs(j + 5, 0)

        u = order(j, 2 * start, nu)
        await_chunk(jnp.where(2 * start + j < nu, u + 1, u))
        hidden_unit(u)

    def out_remote(b, chan):
        return pltpu.make_async_remote_copy(
            src_ref=obuf.at[b, chan],
            dst_ref=out.at[:, pl.ds(yb * s, yb)],
            send_sem=osend.at[b, chan],
            recv_sem=orecv.at[s],
            device_id=dev(nb * c + b, chan),
            device_id_type=MESH,
        )

    def out_local(b):
        return pltpu.make_async_copy(
            obuf.at[b, c], out.at[:, pl.ds(yb * s, yb)], olocal
        )

    def away(b, chan):
        return (nb * c + b != s) | (chan != c)

    def block_step(k, carry):
        lax.fori_loop(
            2 * k + jnp.where(k == 0, 0, 1), 2 * k + 3,
            lambda j, x: (hidden_step(j), x)[1], 0,
        )

        @pl.when(k == 0)
        def _():
            load2.wait()

        b = order(k, start, nb)
        result = convolve(
            [
                hid[pl.ds(slab * b + a, slab), e : e + yb]
                for a in range(3)
                for e in range(3)
            ],
            w2, bias2, slab * yb * zc,
        )
        for chan in range(2):
            obuf[b, chan] = result[:, chan * share : (chan + 1) * share].reshape(
                slab, yb, zc, share
            )
        for chan in range(2):
            @pl.when(away(b, chan))
            def _():
                out_remote(b, chan).start()

        @pl.when(nb * c + b == s)
        def _():
            out_local(b).start()
        return carry

    lax.fori_loop(0, nb, block_step, 0)

    def sent_inputs(q, carry):
        @pl.when(valid(q, other))
        def _():
            partner_in(q).wait_send()

        for way in range(2):
            @pl.when(has(way))
            def _():
                for chan in range(2):
                    @pl.when(valid(q, chan))
                    def _():
                        halo_in(q, way, chan).wait_send()
        return carry

    lax.fori_loop(0, nq, sent_inputs, 0)

    def sent_outputs(b, carry):
        for chan in range(2):
            @pl.when(away(b, chan))
            def _():
                out_remote(b, chan).wait_send()

        @pl.when(nb * c + b == s)
        def _():
            out_local(b).wait()
        return carry

    lax.fori_loop(0, nb, sent_outputs, 0)

    def arrived(i, carry):
        @pl.when((i != s) | (s // nb != c))
        def _():
            region = out.at[:, pl.ds(yb * i, yb)]
            pltpu.make_async_remote_copy(
                src_ref=region,
                dst_ref=region,
                send_sem=osend.at[0, 0],
                recv_sem=orecv.at[i],
                device_id=dev(s, other),
                device_id_type=MESH,
            ).wait_recv()
        return carry

    lax.fori_loop(0, slabs, arrived, 0)


def body(slabs, volume, weight_one, bias_one, weight_two, bias_two):
    rows, yb, zc, share = volume.shape
    half, slab = rows // 2, rows // slabs
    nb = half // slab
    nq = (half + 4) // CHUNK
    channels = weight_one.shape[-1]
    anywhere = pl.BlockSpec(memory_space=pl.ANY)
    vmem = pl.BlockSpec(memory_space=pltpu.VMEM)
    dma = pltpu.SemaphoreType.DMA
    kind = volume.dtype
    return pl.pallas_call(
        functools.partial(kernel, slabs),
        out_shape=jax.ShapeDtypeStruct((slab, yb * slabs, zc, share), kind),
        in_specs=[anywhere, anywhere, anywhere, vmem, vmem],
        out_specs=anywhere,
        scratch_shapes=[
            pltpu.VMEM((2, half + 4, yb + 4, zc, share), kind),
            pltpu.VMEM((half + 2, yb + 2, zc, channels), kind),
            pltpu.VMEM(weight_one.shape, kind),
            pltpu.VMEM(weight_two.shape, kind),
            pltpu.VMEM((nb, 2, slab, yb, zc, share), kind),
            dma((2,)),
            dma((nq,)),
            dma((nq,)),
            dma((nq,)),
            dma((2, 2, nq)),
            dma((2, 2, nq)),
            dma((nb, 2)),
            dma((slabs,)),
            dma,
        ],
        compiler_params=pltpu.CompilerParams(
            collective_id=0, has_side_effects=True, vmem_limit_bytes=58 * 2**20
        ),
    )(volume, weight_one, weight_two, bias_one[None], bias_two[None])


def solution(mesh):
    return jax.shard_map(
        functools.partial(body, mesh.shape["space"]),
        mesh=mesh,
        in_specs=(P(None, "space", "tiles", "chan"), P(), P(), P(), P()),
        out_specs=P("space", None, "tiles", "chan"),
        check_vma=False,
    )
```
